256 devices in a mesh: row: 16 (over y_lo, z), vec: 16 (over y_hi, x, core).
Axes of the slice: x: 4, y: 4 (y_hi: 2, y_lo: 2; y = y_hi * 2 + y_lo), z: 8, core: 2. Of those that a mesh axis runs over, the one named last changes fastest.
Arguments:
- vectors: float32 [16384, 6144], P('row', 'vec'), may hold values from -6 to 6
- reflectors: float32 [64, 512, 256], P('row', 'vec'), may hold values from -0.25 to 0.25
- inner_factors: float32 [64, 256, 256], P('row', 'vec'), may hold values from -0.375 to 0.375
- offsets: int32 [2, 32], P(None, 'row'), may hold values from 0 to 15872, as said below
- owners: int32 [2, 32], P(None, 'row'), may hold values from 0 to 3, as said below
Outputs:
- result: float32 [16384, 6144], P('row', 'vec')
The draws below stay inside these ranges and needn't reach their ends.
Inputs may be any that keep to these rules, and one draw needn't show every extreme that they name: `offsets`: within each sweep the columns j * 2 to (j + 1) * 2 - 1 belong to panel j, the rows j * 1024 to (j + 1) * 1024 - 1; a panel's start rows increase and are multiples of 256. A first-sweep block lies within its panel. A second-sweep block starts 256 rows or more after its panel's first row; in every panel but the last, the last second-sweep block starts at the panel's end minus 256, so it runs 256 rows into the next panel; the last panel's second-sweep blocks lie within it. `owners`: for each panel, its 4 entries (both sweeps) are a permutation of 0 to 3.
All inputs are finite; a program needn't handle non-finite values.
Results may differ from the reference program's by a relative error of at most 0.0001.
Values sent between devices are 32-bit elements; how exact they have to be, the bound alone decides.
No kernel may reach another device: no remote copies, remote signals or barrier semaphores. Data moves between devices by JAX's collectives and lax.ppermute only.
A program may use at most 64 MiB of HBM per device.

```python
import jax
import jax.numpy as jnp
from jax import lax

M = 6144
BROWS = 512
NREF = 256
BPS = 2
ROWS_DEV = 1024
N = 16384
NBLK = 32
STORED = 64


def choose(key, pool, take):
    order = jax.random.permutation(key, pool).astype(jnp.int32)
    return jnp.sort(order[:take])


def draw_offsets(key, part):
    key = jax.random.fold_in(key, 7)
    steps_dev = ROWS_DEV // NREF
    panels = NBLK // BPS

    def one_panel(panel_index):
        first_key = jax.random.fold_in(key, 2 * panel_index)
        second_key = jax.random.fold_in(key, 2 * panel_index + 1)
        middle = choose(first_key, steps_dev - 3, BPS - 2) + 1
        first_sweep = jnp.concatenate([jnp.zeros((1,), jnp.int32), middle, jnp.full((1,), steps_dev - 2, jnp.int32)])
        regular_steps = jnp.concatenate([choose(second_key, steps_dev - 2, BPS - 1) + 1, jnp.full((1,), steps_dev - 1, jnp.int32)])
        final_steps = jnp.concatenate([choose(second_key, steps_dev - 3, BPS - 1) + 1, jnp.full((1,), steps_dev - 2, jnp.int32)])
        second_sweep = jnp.where(panel_index == panels - 1, final_steps, regular_steps)
        both = jnp.stack([first_sweep, second_sweep]) * NREF + panel_index * ROWS_DEV
        return both.astype(jnp.int32)
    stacked = jax.vmap(one_panel)(jnp.arange(panels, dtype=jnp.int32))
    return jnp.transpose(stacked, (1, 0, 2)).reshape(2, NBLK)


def draw_owners(key, part):
    key = jax.random.fold_in(key, 11)
    panels = NBLK // BPS

    def one_panel(panel_index):
        order = jax.random.permutation(jax.random.fold_in(key, panel_index), 2 * BPS)
        return order.astype(jnp.int32).reshape(2, BPS)
    stacked = jax.vmap(one_panel)(jnp.arange(panels, dtype=jnp.int32))
    return jnp.transpose(stacked, (1, 0, 2)).reshape(2, NBLK)


def level_of(own_key, shape, split, least, high):
    factor_of = 1.0
    for axis_at, blocks in split:
        draws = jax.random.uniform(jax.random.fold_in(jax.random.fold_in(own_key, 6), axis_at), (blocks,), jnp.float32, least / len(split), high / len(split))
        factor_of = factor_of * jnp.repeat(jnp.exp(draws), shape[axis_at] // blocks).reshape((-1,) + (1,) * (len(shape) - 1 - axis_at))
    return factor_of


def normal_values(rng, shape, scale, bound, shards=(), held_as=jnp.bfloat16):
    factor_of = level_of(rng, shape, shards, -0.22, 0.18) if shards else 1.0
    result = jax.random.normal(rng, shape, jnp.float32) * scale * factor_of
    return jnp.minimum(jnp.maximum(result, -bound), bound).astype(held_as)


def setup_inputs(seed: int = 0) -> dict:
    arg_keys = jax.random.split(jax.random.key(seed), 6)
    vectors = normal_values(arg_keys[0], (N, M), 1.0, 6.0, ((0, 16), (1, 16)), jnp.float32)
    reflectors = normal_values(arg_keys[1], (STORED, BROWS, NREF), BROWS ** -0.5, 0.25, ((0, 16), (1, 16)), jnp.float32)
    inner_factors = normal_values(arg_keys[2], (STORED, NREF, NREF), NREF ** -0.5, 0.375, ((0, 16), (1, 16)), jnp.float32)
    offsets = draw_offsets(jax.random.fold_in(arg_keys[5], 71), 0)
    owners = draw_owners(jax.random.fold_in(arg_keys[5], 71), 0)
    return dict(vectors=vectors, reflectors=reflectors, inner_factors=inner_factors, offsets=offsets, owners=owners)


def contract_rows(left, right):
    return lax.dot_general(left, right, (((0,), (0,)), ((), ())), precision=lax.Precision.HIGHEST, preferred_element_type=jnp.float32)


def multiply(left, right):
    return jnp.dot(left, right, precision=lax.Precision.HIGHEST, preferred_element_type=jnp.float32)


def reference(vectors, reflectors, inner_factors, offsets, owners):
    def make_sweep(sweep_index):
        def apply_block(block_index, current):
            block_index = jnp.asarray(block_index).astype(jnp.int32)
            start_row = offsets[sweep_index, block_index].astype(jnp.int32)
            stored_at = ((block_index // BPS) * (2 * BPS) + owners[sweep_index, block_index]).astype(jnp.int32)
            basis_block = lax.dynamic_index_in_dim(reflectors, stored_at, 0, keepdims=False)
            inner_block = lax.dynamic_index_in_dim(inner_factors, stored_at, 0, keepdims=False)
            window = lax.dynamic_slice_in_dim(current, start_row, BROWS, 0)
            projection = contract_rows(basis_block, window)
            coupled = multiply(inner_block, projection)
            window = window - multiply(basis_block, coupled)
            return lax.dynamic_update_slice_in_dim(current, window, start_row, 0)
        return apply_block

    current = vectors
    for sweep_index in range(2):
        current = lax.fori_loop(0, NBLK, make_sweep(sweep_index), current)
    return current
```

```python
import functools

import jax
import jax.numpy as jnp
from jax import lax
from jax.experimental import pallas as pl
from jax.experimental.pallas import tpu as pltpu
from jax.sharding import PartitionSpec as P

ROW, VEC = "row", "vec"
Y, X, C = 2, 4, 2
FIRST = 1
BASIS, INNER = 32, 16
PIECE = BASIS + INNER
STEP = 256
ROWS = 1024
VMEM = pl.BlockSpec(memory_space=pltpu.VMEM)
SMEM = pl.BlockSpec(memory_space=pltpu.SMEM)
ANY = pl.BlockSpec(memory_space=pl.ANY)


def index_of(y, x, c):
    return (y * X + x) * C + c


def routes(target):
    pairs = []
    for y in range(Y):
        for x in range(X):
            for c in range(C):
                ty, tx, tc = target(y, x, c)
                pairs.append((index_of(y, x, c), index_of(ty % Y, tx % X, tc)))
    return pairs


def side(c):
    return 1 - 2 * c


SWAP = routes(lambda y, x, c: (y, x, 1 - c))
NEAR = routes(lambda y, x, c: (y, x + side(c), c))
CROSS = routes(lambda y, x, c: (y + 1, x + side(c), c))
FAR = routes(lambda y, x, c: (y, x + 2, c) if c == 0 else (y + 1, x, c))
LAST = routes(lambda y, x, c: (y + 1, x + 2, c))


def send(block, route):
    return lax.ppermute(block, VEC, route)


def collect(own, other):
    chip = jnp.concatenate([own, other], 0)
    received = [send(chip, NEAR), send(chip, CROSS), send(chip, FAR), send(own, LAST)]
    swapped = [send(block, SWAP) for block in received]
    return [own, other, *received, *swapped]


def sources(vec):
    c = lax.rem(vec, C)
    x = lax.rem(vec // C, X)
    y = vec // (C * X)
    d = side(c)

    def at(dy, dx, dc):
        return index_of(lax.rem(y + dy, Y), lax.rem(x + dx + X, X), lax.rem(c + dc, C))

    far_y, far_x = c, 2 - 2 * c
    return [
        [at(0, 0, 0)],
        [at(0, 0, 1)],
        [at(0, -d, 0), at(0, -d, 1)],
        [at(1, -d, 0), at(1, -d, 1)],
        [at(far_y, far_x, 0), at(far_y, far_x, 1)],
        [at(1, 2, 0)],
        [at(0, d, 1), at(0, d, 0)],
        [at(1, d, 1), at(1, d, 0)],
        [at(1 - far_y, 2 - far_x, 1), at(1 - far_y, 2 - far_x, 0)],
        [at(1, 2, 1)],
    ]


def split(value):
    high = value.astype(jnp.bfloat16)
    low = (value - high.astype(jnp.float32)).astype(jnp.bfloat16)
    return high, low


def product(left, right, dims):
    dot = functools.partial(
        lax.dot_general, dimension_numbers=(dims, ((), ())), preferred_element_type=jnp.float32
    )
    return dot(left[0], right[0]) + (dot(left[0], right[1]) + dot(left[1], right[0]))


def order_kernel(owners, reflectors, inner, out):
    for sweep in range(2):
        for block in range(2):
            code = owners[sweep, block]
            at = (sweep * 2 + block) * PIECE
            out[at : at + BASIS] = reflectors[code]
            out[at + BASIS : at + PIECE] = inner[code]


def apply_blocks(first_row, vec, starts, pieces, work, basis, inner, b0=0):
    places = sources(vec)
    n_blocks = len(starts)
    for b in range(n_blocks):
        for ref, owners in zip(pieces, places, strict=True):
            rows = ref.shape[0] // len(owners)
            for i, device in enumerate(owners):
                at = i * rows + b * PIECE
                high, low = split(ref[at : at + PIECE, :])
                to = pl.ds(pl.multiple_of(device * BASIS, BASIS), BASIS)
                basis[b, 0, to, :] = high[:BASIS]
                basis[b, 1, to, :] = low[:BASIS]
                to = pl.ds(pl.multiple_of(device * INNER, INNER), INNER)
                inner[b, 0, to, :] = high[BASIS:]
                inner[b, 1, to, :] = low[BASIS:]
    for b, start in enumerate(starts):
        window = pl.ds(pl.multiple_of(start - first_row, STEP), 2 * STEP)
        v = (basis[b, 0], basis[b, 1])
        s = (inner[b, 0], inner[b, 1])
        old = work[window, :]
        projection = product(v, split(old), ((0,), (0,)))
        coupled = product(s, split(projection), ((1,), (0,)))
        work[window, :] = old - product(v, split(coupled), ((1,), (0,)))


def first_kernel(n, position, offsets, vectors, *refs):
    pieces, (out, head, basis, inner) = refs[:-4], refs[-4:]
    out[...] = vectors[...]
    starts = [offsets[b // 2, b % 2] for b in range(n)]
    apply_blocks(position[0] * ROWS, position[1], starts, pieces, out, basis, inner)
    head[...] = out[:STEP, :]


def second_kernel(n, position, offsets, vectors, below, *refs):
    pieces, (out, handed, work, basis, inner) = refs[:-5], refs[-5:]
    work[:ROWS, :] = vectors[...]
    work[ROWS:, :] = below[...]
    starts = [offsets[b // 2, b % 2] for b in range(4 - n, 4)]
    apply_blocks(position[0] * ROWS, position[1], starts, pieces, work, basis, inner)
    handed[...] = work[ROWS:, :]
    out[...] = work[:ROWS, :]


def finish_kernel(position, handed, body, out, sem):
    del body

    @pl.when(position[0] > 0)
    def _():
        copy = pltpu.make_async_copy(handed, out.at[:STEP, :], sem)
        copy.start()
        copy.wait()


def neighbour(block, step):
    size = lax.axis_size(ROW)
    return lax.ppermute(block, ROW, [(i, i + step) for i in range(size) if 0 <= i + step < size])


def shards(vectors, reflectors, inner_factors, offsets, owners):
    columns = vectors.shape[1]
    f32 = jnp.float32
    position = jnp.stack([lax.axis_index(ROW), lax.axis_index(VEC)]).astype(jnp.int32)

    def scratch(n):
        return [
            pltpu.VMEM((n, 2, 2 * STEP, STEP), jnp.bfloat16),
            pltpu.VMEM((n, 2, STEP, STEP), jnp.bfloat16),
        ]

    def cost(n):
        return pl.CostEstimate(flops=n * 3 * 250_000_000, bytes_accessed=4_000_000, transcendentals=0)

    own = pl.pallas_call(
        order_kernel,
        out_shape=jax.ShapeDtypeStruct((4 * PIECE, STEP), f32),
        in_specs=[SMEM, VMEM, VMEM],
        out_specs=VMEM,
    )(owners, reflectors, inner_factors)
    cut = FIRST * PIECE
    other = send(own, SWAP)
    early = collect(own[:cut], other[:cut])
    late = collect(own[cut:], other[cut:])

    n = FIRST
    current, head = pl.pallas_call(
        functools.partial(first_kernel, n),
        out_shape=(jax.ShapeDtypeStruct(vectors.shape, f32), jax.ShapeDtypeStruct((STEP, columns), f32)),
        in_specs=[SMEM, SMEM, VMEM] + [VMEM] * len(early),
        out_specs=(VMEM, VMEM),
        scratch_shapes=scratch(n),
        cost_estimate=cost(n),
    )(position, offsets, vectors, *early)
    below = neighbour(head, -1)

    n = 4 - FIRST
    body, handed = pl.pallas_call(
        functools.partial(second_kernel, n),
        out_shape=(jax.ShapeDtypeStruct(vectors.shape, f32), jax.ShapeDtypeStruct((STEP, columns), f32)),
        in_specs=[SMEM, SMEM, VMEM, VMEM] + [VMEM] * len(late),
        out_specs=(VMEM, VMEM),
        scratch_shapes=[pltpu.VMEM((ROWS + STEP, columns), f32)] + scratch(n),
        cost_estimate=cost(n),
    )(position, offsets, current, below, *late)
    arrived = neighbour(handed, 1)

    return pl.pallas_call(
        finish_kernel,
        out_shape=jax.ShapeDtypeStruct(vectors.shape, f32),
        in_specs=[SMEM, ANY, ANY],
        out_specs=ANY,
        scratch_shapes=[pltpu.SemaphoreType.DMA],
        input_output_aliases={2: 0},
    )(position, arrived, body)


def solution(mesh):
    return jax.shard_map(
        shards,
        mesh=mesh,
        in_specs=(
            P(ROW, VEC),
            P(ROW, VEC, None),
            P(ROW, VEC, None),
            P(None, ROW),
            P(None, ROW),
        ),
        out_specs=P(ROW, VEC),
        check_vma=False,
    )
```
